128 devices in a mesh: row: 8 (over y, core), col: 16 (over x, z).
Axes of the slice: x: 4, y: 4, z: 4, core: 2. Of those that a mesh axis runs over, the one named last changes fastest.
Arguments:
- rhs_low: bfloat16 [32768, 512], P(('row', 'col')), may hold values from -6 to 6
- rhs_top: bfloat16 [16384, 512], P('row'), may hold values from -6 to 6
- lower_blocks: bfloat16 [128, 256, 128, 128], P('row', 'col'), may hold values from -0.03125 to 0.03125
- upper_blocks: bfloat16 [128, 256, 128, 128], P('row', 'col'), may hold values from -0.046875 to 0.046875
- block_target: int32 [128, 256], P('row', 'col'), may hold values from 0 to 15
- inv_lower_low: bfloat16 [256, 128, 128], P(('row', 'col')), as said below
- inv_upper_low: bfloat16 [256, 128, 128], P(('row', 'col')), as said below
- inv_lower_top: bfloat16 [128, 128, 128], P('row'), as said below
- inv_upper_top: bfloat16 [128, 128, 128], P('row'), as said below
Outputs:
- sol_low: bfloat16 [32768, 512], P(('row', 'col'))
- sol_top: bfloat16 [16384, 512], P(('row', 'col'))
The draws below stay inside these ranges and needn't reach their ends.
Inputs may be any that keep to these rules, and one draw needn't show every extreme that they name: `inv_lower_low`: lower triangular with nonzero diagonal. `inv_upper_low`: upper triangular with nonzero diagonal. `inv_lower_top`: lower triangular with nonzero diagonal. `inv_upper_top`: upper triangular with nonzero diagonal.
All inputs are finite; a program needn't handle non-finite values.
Results may differ from the reference program's by a relative error of at most 0.024.
Values may be sent and summed in bfloat16 or wider, within the bound.
A program may use at most 128 MiB of HBM per device.

```python
import math
import jax
import jax.numpy as jnp
from jax import lax

B = 128
NRHS = 512
E = 16
K1R = 2
P2D = 1
N1 = 256
P2 = 16
N2 = 128
EROWS = 128
N_ROW = 8
N_COL = 16


def triangular(key, count, lower):
    values = jax.random.normal(key, (count, B, B), jnp.float32) * (1.5 / math.sqrt(B))
    scales = jax.random.uniform(jax.random.fold_in(key, 7), (count, B, B), jnp.float32, 0.5, 2.0)
    rows = lax.broadcasted_iota(jnp.int32, (B, B), 0)
    cols = lax.broadcasted_iota(jnp.int32, (B, B), 1)
    if lower:
        keep = rows > cols
    else:
        keep = rows < cols
    return jnp.where(keep[None], values, jnp.where((rows == cols)[None], scales, 0.0))


def draw_inv_lower_low(key, part):
    return triangular(jax.random.fold_in(key, 11), N1, True).astype(jnp.bfloat16)


def draw_inv_upper_low(key, part):
    return triangular(jax.random.fold_in(key, 12), N1, False).astype(jnp.bfloat16)


def draw_inv_lower_top(key, part):
    return triangular(jax.random.fold_in(key, 13), N2, True).astype(jnp.bfloat16)


def draw_inv_upper_top(key, part):
    return triangular(jax.random.fold_in(key, 14), N2, False).astype(jnp.bfloat16)


def touch_ends(drawn, rng, low, top_value):
    spot = [jax.random.randint(jax.random.fold_in(rng, axis), (), 0, length) for axis, length in enumerate(drawn.shape)]
    main_axis = drawn.shape.index(max(drawn.shape))
    next_to = spot[:main_axis] + [(spot[main_axis] + 1) % drawn.shape[main_axis]] + spot[main_axis + 1:]
    return drawn.at[tuple(spot)].set(low).at[tuple(next_to)].set(top_value)


def shard_levels(key, dims, shards, smallest, high):
    level, own = 1.0, jax.random.fold_in(key, 6)
    for dim, shards_of in shards:
        steps = jnp.exp(jax.random.uniform(jax.random.fold_in(own, dim), (shards_of,), jnp.float32, smallest / len(shards), high / len(shards)))
        level = level * jnp.repeat(steps, dims[dim] // shards_of).reshape([-1 if axis == dim else 1 for axis in range(len(dims))])
    return level


def gaussian(own_key, dims, deviation, limit, cuts=(), kind=jnp.bfloat16):
    values = deviation * jax.random.normal(own_key, dims, jnp.float32)
    if cuts:
        values = values * shard_levels(own_key, dims, cuts, -0.22, 0.18)
    return jnp.clip(values, -limit, limit).astype(kind)


def setup_inputs(seed: int = 0) -> dict:
    key_list = jax.random.split(jax.random.key(seed), 10)
    return {
        "rhs_low": gaussian(key_list[0], (N1 * B, NRHS), 1.0, 6.0, ((0, 128),)),
        "rhs_top": gaussian(key_list[1], (N2 * B, NRHS), 1.0, 6.0, ((0, 8),)),
        "lower_blocks": gaussian(key_list[2], (EROWS, N1, B, B), (B * E * K1R * N_ROW // P2D) ** -0.5, 0.03125, ((0, 8), (1, 16))),
        "upper_blocks": gaussian(key_list[3], (EROWS, N1, B, B), (B * E * N_ROW) ** -0.5, 0.046875, ((0, 8), (1, 16))),
        "block_target": touch_ends(jax.random.randint(key_list[4], (EROWS, N1), 0, P2), jax.random.fold_in(key_list[4], 1), 0, P2 - 1).astype(jnp.int32),
        "inv_lower_low": draw_inv_lower_low(jax.random.fold_in(key_list[9], 71), 0),
        "inv_upper_low": draw_inv_upper_low(jax.random.fold_in(key_list[9], 71), 0),
        "inv_lower_top": draw_inv_lower_top(jax.random.fold_in(key_list[9], 71), 0),
        "inv_upper_top": draw_inv_upper_top(jax.random.fold_in(key_list[9], 71), 0),
    }


def forward_partial(row, col, fwd_grid, lower_blocks, block_target):
    column = lax.dynamic_index_in_dim(fwd_grid, col, 1, keepdims=False).reshape(N_ROW * K1R, B, NRHS)
    blocks = lax.dynamic_slice_in_dim(lax.dynamic_slice_in_dim(lower_blocks, row * E, E, 0), col * (N_ROW * K1R), N_ROW * K1R, 1)
    targets = lax.dynamic_slice_in_dim(lax.dynamic_slice_in_dim(block_target, row * E, E, 0), col * (N_ROW * K1R), N_ROW * K1R, 1)
    slots = jnp.arange(P2D * N_COL, dtype=jnp.int32)
    column_f = column.astype(jnp.float32)

    def step(total, item):
        blk, tgt = item
        prod = jnp.einsum('kab,kbj->kaj', blk.astype(jnp.float32), column_f)
        onehot = (tgt[:, None] == slots[None, :]).astype(jnp.float32)
        return total + jnp.einsum('kp,kaj->paj', onehot, prod, precision=lax.Precision.HIGHEST), None

    start = jnp.zeros((P2D * N_COL, B, NRHS), jnp.float32)
    total, _ = lax.scan(step, start, (blocks, targets))
    return total.astype(jnp.bfloat16)


def backward_partial(row, col, top_grid, upper_blocks, block_target):
    solved = lax.dynamic_index_in_dim(top_grid, row, 0, keepdims=False)
    blocks = lax.dynamic_slice_in_dim(lax.dynamic_slice_in_dim(upper_blocks, row * E, E, 0), col * (N_ROW * K1R), N_ROW * K1R, 1)
    targets = lax.dynamic_slice_in_dim(lax.dynamic_slice_in_dim(block_target, row * E, E, 0), col * (N_ROW * K1R), N_ROW * K1R, 1)

    def step(total, item):
        blk, tgt = item
        picked = jnp.take(solved, tgt, axis=0).astype(jnp.float32)
        return total + jnp.einsum('kab,kbj->kaj', blk.astype(jnp.float32), picked), None

    start = jnp.zeros((N_ROW * K1R, B, NRHS), jnp.float32)
    total, _ = lax.scan(step, start, (blocks, targets))
    return total.astype(jnp.bfloat16)


def reference(rhs_low, rhs_top, lower_blocks, upper_blocks, block_target, inv_lower_low, inv_upper_low, inv_lower_top, inv_upper_top):
    count_low = K1R * N_ROW * N_COL
    count_top = P2D * N_COL * N_ROW
    rhs_blocks = rhs_low.reshape(count_low, B, NRHS).astype(jnp.float32)
    fwd_low = jnp.einsum('kab,kbj->kaj', inv_lower_low.astype(jnp.float32), rhs_blocks).astype(jnp.bfloat16)
    fwd_grid = fwd_low.reshape(N_ROW, N_COL, K1R, B, NRHS)
    rows = jnp.arange(N_ROW, dtype=jnp.int32)
    cols = jnp.arange(N_COL, dtype=jnp.int32)

    def row_sum(row):
        parts = lax.map(lambda col: forward_partial(row, col, fwd_grid, lower_blocks, block_target), cols)
        return jnp.sum(parts.astype(jnp.float32), axis=0)

    lsum = lax.map(row_sum, rows).reshape(count_top, B, NRHS)
    resid_top = (rhs_top.reshape(count_top, B, NRHS).astype(jnp.float32) - lsum).astype(jnp.bfloat16)
    fwd_top = jnp.einsum('kab,kbj->kaj', inv_lower_top.astype(jnp.float32), resid_top.astype(jnp.float32)).astype(jnp.bfloat16)
    sol_top = jnp.einsum('kab,kbj->kaj', inv_upper_top.astype(jnp.float32), fwd_top.astype(jnp.float32)).astype(jnp.bfloat16)
    top_grid = sol_top.reshape(N_ROW, P2D * N_COL, B, NRHS)

    def col_sum(col):
        parts = lax.map(lambda row: backward_partial(row, col, top_grid, upper_blocks, block_target), rows)
        return jnp.sum(parts.astype(jnp.float32), axis=0)

    usum = lax.map(col_sum, cols).reshape(N_COL, N_ROW, K1R, B, NRHS)
    usum = jnp.transpose(usum, (1, 0, 2, 3, 4)).reshape(count_low, B, NRHS)
    resid_low = (fwd_low.astype(jnp.float32) - usum).astype(jnp.bfloat16)
    sol_low = jnp.einsum('kab,kbj->kaj', inv_upper_low.astype(jnp.float32), resid_low.astype(jnp.float32)).astype(jnp.bfloat16)
    return sol_low.reshape(count_low * B, NRHS), sol_top.reshape(count_top * B, NRHS)
```

```python
import functools

import jax
import jax.numpy as jnp
from jax import lax
from jax.experimental import pallas as pl
from jax.experimental.pallas import tpu as pltpu
from jax.sharding import PartitionSpec as P

RING = 4
CHUNKS = 2
BF, F32 = jnp.bfloat16, jnp.float32
MESH = pl.DeviceIdType.MESH


def wrap(i):
    return lax.rem(i + RING, RING)


def dot(a, b):
    return jnp.dot(a, b, preferred_element_type=F32)


def kernel(
    names,
    tbl,
    rhs_low,
    rhs_top,
    lower,
    upper,
    inv_ll,
    inv_ul,
    inv_lt,
    inv_ut,
    out_low,
    out_top,
    *scratch,
):
    s = dict(zip(names, scratch))
    slots, positions, B, _ = lower.shape
    n = s["fwd"].shape[2]
    half = B // 2
    r, c = lax.axis_index("row"), lax.axis_index("col")
    y, core = lax.div(r, 2), lax.rem(r, 2)
    x, z = lax.div(c, RING), lax.rem(c, RING)
    partner = (y * 2 + 1 - core, c)

    def y_at(d):
        return (wrap(y + d) * 2 + core, c)

    def x_at(d):
        return (r, wrap(x + d) * RING + z)

    def z_at(d):
        return (r, x * RING + wrap(z + d))

    barrier = pltpu.get_barrier_semaphore()
    neighbours = [partner] + [at(d) for at in (y_at, x_at, z_at) for d in (1, -1)]
    for device in neighbours:
        pl.semaphore_signal(barrier, inc=1, device_id=device, device_id_type=MESH)

    local_count = [0]
    local_open = []

    def local(src, dst):
        copy = pltpu.make_async_copy(src, dst, s["local_sem"].at[local_count[0]])
        local_count[0] += 1
        copy.start()
        return copy

    small = [
        local(rhs_low, s["rhs_low"]),
        local(inv_ll, s["inv_ll"]),
    ]
    group = positions // 4
    lower_in = [
        local(lower.at[:, pl.ds(g * group, group)], s["low_in"].at[:, pl.ds(g * group, group)])
        for g in range(4)
    ]
    top_in = [
        local(rhs_top.at[pl.ds(pl.multiple_of(c * B, B), B)], s["rhs_top"]),
        local(inv_lt.at[c], s["inv_lt"]),
        local(inv_ut.at[c], s["inv_ut"]),
        local(inv_ul, s["inv_ul"]),
    ]
    upper_in = [
        local(upper.at[:, pl.ds(g * group, group)], s["up_in"].at[:, pl.ds(g * group, group)])
        for g in range(4)
    ]

    remote_ids = {}
    sends = []

    def remote_id(key):
        return remote_ids.setdefault(key, len(remote_ids))

    def send(key, src, dst, device):
        i = remote_id(key)
        copy = pltpu.make_async_remote_copy(
            src_ref=src,
            dst_ref=dst,
            send_sem=s["send_sem"].at[i],
            recv_sem=s["recv_sem"].at[i],
            device_id=device,
            device_id_type=MESH,
        )
        copy.start()
        sends.append(copy)

    def arrive(key, dst):
        i = remote_id(key)
        pltpu.make_async_remote_copy(
            src_ref=dst,
            dst_ref=dst,
            send_sem=s["send_sem"].at[i],
            recv_sem=s["recv_sem"].at[i],
            device_id=partner,
            device_id_type=MESH,
        ).wait_recv()

    for copy in small:
        copy.wait()

    def own_rows(row):
        return pl.ds(pl.multiple_of(row * (2 * B), 2 * B), 2 * B)

    def own_half(row, j):
        return pl.ds(pl.multiple_of(row * (2 * B) + j * B, B), B)

    for j in range(2):
        solved = dot(s["inv_ll"][j], s["rhs_low"][pl.ds(j * B, B)]).astype(BF)
        for k in range(CHUNKS):
            s["fwd"][k, own_half(r, j)] = solved[:, k * n : (k + 1) * n]

    pl.semaphore_wait(barrier, len(neighbours))

    s["sum_a"][0] = jnp.zeros((B, B), F32)
    s["sum_b"][0] = jnp.zeros((B, B), F32)

    def build(source, arrivals, write):
        hop = positions // 2
        pending = list(arrivals)

        def one(acc, m):
            for e in range(slots):
                before = tbl[e * positions + m]
                acc[e + 1] = source[e, m].astype(F32) + acc[before]

        def put(acc, m):
            for q in range(slots):
                last = tbl[(slots + q) * positions + m]
                write(q, m, acc[last].astype(BF))

        def step(i, carry):
            m0, m1 = 2 * i, 2 * i + 1
            one(s["sum_a"], m0)
            one(s["sum_b"], m1)
            put(s["sum_a"], m0)
            put(s["sum_b"], m1)
            return carry

        per = group // 2
        for g in range(4):
            pending[g].wait()
            lax.fori_loop(g * per, (g + 1) * per, step, 0)
            yield

    def write_low(q, m, value):
        s["low"][q // RING, q % RING, :, pl.ds(pl.multiple_of(m * B, B), B)] = value

    def write_up(q, m, value):
        s["up"][m, :, pl.ds(q * B, B)] = value

    low_build = build(s["low_in"], lower_in, write_low)
    up_build = build(s["up_in"], upper_in, write_up)

    def builds():
        yield from low_build
        yield from up_build

    building = builds()

    def finish(gen):
        for _ in gen:
            pass

    def reduce_ring(tag, k, at, piece, name):
        s1, r1 = s[name + "_s1"].at[k], s[name + "_r1"].at[k]
        s2, r2 = s[name + "_s2"].at[k], s[name + "_r2"].at[k]
        acc = s[name + "_acc"].at[k]
        s1[...] = piece(2).astype(BF)
        send((tag, "far", 1), s1.at[0], r1.at[0], at(1))
        send((tag, "far", -1), s1.at[1], r1.at[1], at(-1))
        acc[0] = piece(1)
        s2[0, 1] = acc[0, 1].astype(BF)
        send((tag, "near", 1), s2.at[0, 1], r2.at[0, 1], at(1))
        acc[1] = piece(-1)
        s2[1, 0] = acc[1, 0].astype(BF)
        send((tag, "near", -1), s2.at[1, 0], r2.at[1, 0], at(-1))
        acc[2] = piece(0)
        yield
        arrive((tag, "far", 1), r1.at[0])
        s2[0, 0] = (acc[0, 0] + r1[0].astype(F32)).astype(BF)
        send((tag, "sum", 1), s2.at[0, 0], r2.at[0, 0], at(1))
        arrive((tag, "far", -1), r1.at[1])
        s2[1, 1] = (acc[1, 1] + r1[1].astype(F32)).astype(BF)
        send((tag, "sum", -1), s2.at[1, 1], r2.at[1, 1], at(-1))
        yield
        for step, d, h in (("near", 1, 1), ("near", -1, 0), ("sum", 1, 0), ("sum", -1, 1)):
            arrive((tag, step, d), r2.at[0 if d == 1 else 1, h])
        acc[2] = acc[2] + r2[0].astype(F32) + r2[1].astype(F32)

    def chunk(k):
        heavy_x = k % 2 == 0
        heavy_at, light_at = (x_at, z_at) if heavy_x else (z_at, x_at)
        h, l = (x, z) if heavy_x else (z, x)
        fwd, solved = s["fwd"].at[k], s["solved"].at[k]

        def row_of(d, side):
            return wrap(y + d) * 2 + (core if side == 0 else 1 - core)

        own = fwd.at[own_rows(r)]
        send((k, "gy", 1), own, own, y_at(1))
        send((k, "gy", -1), own, own, y_at(-1))
        send((k, "gc", 0), own, own, partner)
        yield
        before = fwd.at[own_rows(row_of(-1, 0))]
        arrive((k, "gy", 1), before)
        part = fwd.at[own_half(row_of(-1, 0), 0)]
        send((k, "gy2", 1), part, part, y_at(1))
        send((k, "gc", -1), before, before, partner)
        after = fwd.at[own_rows(row_of(1, 0))]
        arrive((k, "gy", -1), after)
        part = fwd.at[own_half(row_of(1, 0), 1)]
        send((k, "gy2", -1), part, part, y_at(-1))
        send((k, "gc", 1), after, after, partner)
        yield
        for j, d in ((0, 1), (1, -1)):
            part = fwd.at[own_half(row_of(2, 0), j)]
            arrive((k, "gy2", d), part)
            send((k, "gc2", j), part, part, partner)
        yield
        finish(low_build)
        for d in (0, -1, 1):
            arrive((k, "gc", d), fwd.at[own_rows(row_of(d, 1))])
        for j in range(2):
            arrive((k, "gc2", j), fwd.at[own_half(row_of(2, 1), j)])

        def top_piece(d):
            p = wrap(h + d)
            rows = s["low"][p] if heavy_x else s["low"][:, p]
            return dot(rows.reshape(RING * B, -1), fwd[...]).reshape(2, 2 * B, n)

        yield from reduce_ring((k, "heavy"), k, heavy_at, top_piece, "heavy")
        summed = s["heavy_acc"]

        def light_piece(d):
            p = wrap(l + d)
            q, t = lax.div(p, 2), lax.rem(p, 2)
            start = pl.multiple_of(t * B, B)
            return summed[k, 2, q, pl.ds(start, B)].reshape(2, half, n)

        yield from reduce_ring((k, "light"), k, light_at, light_piece, "light")
        lsum = s["light_acc"][k, 2].reshape(B, n)

        if k == 0:
            for copy in top_in:
                copy.wait()
        resid_top = (s["rhs_top"][:, k * n : (k + 1) * n].astype(F32) - lsum).astype(BF)
        fwd_top = dot(s["inv_lt"][...], resid_top).astype(BF)
        solved[x, z] = dot(s["inv_ut"][...], fwd_top).astype(BF)
        local_open.append(local(solved.at[x, z], out_top.at[:, pl.ds(k * n, n)]))

        def block(dh, dl):
            a, b = wrap(h + dh), wrap(l + dl)
            return solved.at[a, b] if heavy_x else solved.at[b, a]

        def part_of(ref, i):
            return ref.at[pl.ds(i * half, half)]

        def spread(dl):
            for d in (1, -1):
                send((k, "sh", dl, d), block(0, dl), block(0, dl), heavy_at(d))

        for d in (1, -1):
            send((k, "sl", d), block(0, 0), block(0, 0), light_at(d))
        spread(0)
        yield
        arrive((k, "sl", 1), block(0, -1))
        part = part_of(block(0, -1), 0)
        send((k, "sl2", 1), part, part, light_at(1))
        spread(-1)
        arrive((k, "sl", -1), block(0, 1))
        part = part_of(block(0, 1), 1)
        send((k, "sl2", -1), part, part, light_at(-1))
        spread(1)
        yield
        arrive((k, "sl2", 1), part_of(block(0, 2), 0))
        arrive((k, "sl2", -1), part_of(block(0, 2), 1))
        spread(2)
        for dl in (0, 1):
            arrive((k, "sh", dl, 1), block(-1, dl))
            send((k, "sh2", dl), block(-1, dl), block(-1, dl), heavy_at(1))
        arrive((k, "sh", -1, -1), block(1, -1))
        send((k, "sh2", -1), block(1, -1), block(1, -1), heavy_at(-1))
        yield
        arrive((k, "sh", 2, -1), block(1, 2))
        send((k, "sh2", 2), block(1, 2), block(1, 2), heavy_at(-1))
        yield
        finish(low_build)
        finish(up_build)
        for dl in (-1, 2):
            arrive((k, "sh", dl, 1), block(-1, dl))
        for dl in (0, 1):
            arrive((k, "sh", dl, -1), block(1, dl))
        for dl in (0, 1, -1, 2):
            arrive((k, "sh2", dl), block(2, dl))

        def low_rows(d, side):
            first = pl.multiple_of(row_of(d, side) * 2, 2)
            rows = s["up"][pl.ds(first, 2)].reshape(2 * B, -1)
            return dot(rows, solved[...].reshape(-1, n))

        for d in (2, 1, -1, 0):
            i = d % RING
            s["pair_s"][k, i] = low_rows(d, 1).astype(BF)
            send((k, "pair", d), s["pair_s"].at[k, i], s["pair_r"].at[k, i], partner)
        yield

        def low_piece(d):
            mine = low_rows(d, 0)
            arrive((k, "pair", d), s["pair_r"].at[k, d % RING])
            return (mine + s["pair_r"][k, d % RING].astype(F32)).reshape(2, B, n)

        yield from reduce_ring((k, "low"), k, y_at, low_piece, "row")
        usum = s["row_acc"].at[k, 2]
        for j in range(2):
            resid = (fwd[own_half(r, j)].astype(F32) - usum[j]).astype(BF)
            s["out_low"][k, pl.ds(j * B, B)] = dot(s["inv_ul"][j], resid).astype(BF)
        local_open.append(local(s["out_low"].at[k], out_low.at[:, pl.ds(k * n, n)]))

    live = [chunk(k) for k in range(CHUNKS)]
    while live:
        for gen in list(live):
            if next(gen, "done") == "done":
                live.remove(gen)
            next(building, None)
    for copy in local_open:
        copy.wait()
    for copy in sends:
        copy.wait_send()


def tables(targets):
    slots = targets.shape[0]
    order = jnp.arange(slots, dtype=jnp.int32)
    number = (order + 1)[:, None, None]
    same = targets[:, None, :] == targets[None, :, :]
    earlier = (order[:, None] < order[None, :])[:, :, None]
    before = jnp.max(jnp.where(same & earlier, number, 0), axis=0)
    hit = targets[:, None, :] == order[None, :, None]
    last = jnp.max(jnp.where(hit, number, 0), axis=0)
    return jnp.concatenate([before, last], axis=0).reshape(-1)


def body(
    rhs_low,
    rhs_top,
    lower_blocks,
    upper_blocks,
    block_target,
    inv_lower_low,
    inv_upper_low,
    inv_lower_top,
    inv_upper_top,
):
    slots, positions, B, _ = lower_blocks.shape
    count = rhs_low.shape[1]
    C, n = CHUNKS, rhs_low.shape[1] // CHUNKS
    VM = pltpu.VMEM

    def ring(name, depth):
        return {
            name + "_s1": VM((C, 2, depth, n), BF),
            name + "_r1": VM((C, 2, depth, n), BF),
            name + "_s2": VM((C, 2, 2, depth, n), BF),
            name + "_r2": VM((C, 2, 2, depth, n), BF),
            name + "_acc": VM((C, 3, 2, depth, n), F32),
        }

    scratch = {
        "rhs_low": VM(rhs_low.shape, BF),
        "inv_ll": VM(inv_lower_low.shape, BF),
        "inv_ul": VM(inv_upper_low.shape, BF),
        "rhs_top": VM((B, count), BF),
        "inv_lt": VM((B, B), BF),
        "inv_ut": VM((B, B), BF),
        "low_in": VM(lower_blocks.shape, BF),
        "up_in": VM(upper_blocks.shape, BF),
        "low": VM((RING, RING, B, positions * B), BF),
        "up": VM((positions, B, RING * RING * B), BF),
        "sum_a": VM((slots + 1, B, B), F32),
        "sum_b": VM((slots + 1, B, B), F32),
        "fwd": VM((C, positions * B, n), BF),
        "solved": VM((C, RING, RING, B, n), BF),
        "pair_s": VM((C, RING, 2 * B, n), BF),
        "pair_r": VM((C, RING, 2 * B, n), BF),
        "out_low": VM((C, 2 * B, n), BF),
        **ring("heavy", 2 * B),
        **ring("light", B // 2),
        **ring("row", B),
        "local_sem": pltpu.SemaphoreType.DMA((14 + 2 * C,)),
        "send_sem": pltpu.SemaphoreType.DMA((50 * C,)),
        "recv_sem": pltpu.SemaphoreType.DMA((50 * C,)),
    }
    anywhere = pl.BlockSpec(memory_space=pl.ANY)
    return pl.pallas_call(
        functools.partial(kernel, tuple(scratch)),
        out_shape=(
            jax.ShapeDtypeStruct((2 * B, count), BF),
            jax.ShapeDtypeStruct((B, count), BF),
        ),
        in_specs=[pl.BlockSpec(memory_space=pltpu.SMEM)] + [anywhere] * 8,
        out_specs=(anywhere, anywhere),
        scratch_shapes=list(scratch.values()),
        compiler_params=pltpu.CompilerParams(
            collective_id=0, has_side_effects=True, vmem_limit_bytes=66_000_000
        ),
    )(
        tables(block_target),
        rhs_low,
        rhs_top,
        lower_blocks,
        upper_blocks,
        inv_lower_low,
        inv_upper_low,
        inv_lower_top,
        inv_upper_top,
    )


def solution(mesh):
    placed = (
        P(("row", "col"), None),
        P("row", None),
        P("row", "col", None, None),
        P("row", "col", None, None),
        P("row", "col"),
        P(("row", "col"), None, None),
        P(("row", "col"), None, None),
        P("row", None, None),
        P("row", None, None),
    )
    return jax.shard_map(
        body,
        mesh=mesh,
        in_specs=placed,
        out_specs=(P(("row", "col"), None), P(("row", "col"), None)),
        check_vma=False,
    )
```

```python
import functools
import math

import jax
import jax.numpy as jnp
from jax import lax
from jax.experimental import pallas as pl
from jax.experimental.pallas import tpu as pltpu
from jax.sharding import PartitionSpec as P

RING = 4
NEAR_FIRST = (0, -1, 1, 2)
LIGHT = (1, -1, 2)
GROUPS = 2
LAG = 0
BF, F32 = jnp.bfloat16, jnp.float32
MESH = pl.DeviceIdType.MESH


def wrap(i):
    return lax.rem(i + RING, RING)


def dot(a, b):
    return jnp.dot(a, b, preferred_element_type=F32)


def kernel(
    names,
    target,
    rhs_low,
    rhs_top,
    lower,
    upper,
    inv_ll,
    inv_ul,
    inv_lt,
    inv_ut,
    out_low,
    out_top,
    *scratch,
):
    s = dict(zip(names, scratch))
    slots, positions, B, _ = lower.shape
    n = s["fwd"].shape[2]
    w = n // 2
    r, c = lax.axis_index("row"), lax.axis_index("col")
    y, core = lax.div(r, 2), lax.rem(r, 2)
    x, z = lax.div(c, RING), lax.rem(c, RING)
    partner = (y * 2 + 1 - core, c)

    def y_at(d):
        return (wrap(y + d) * 2 + core, c)

    def x_at(d):
        return (r, wrap(x + d) * RING + z)

    def z_at(d):
        return (r, x * RING + wrap(z + d))

    barrier = pltpu.get_barrier_semaphore()
    neighbours = [partner] + [at(d) for at in (y_at, x_at, z_at) for d in (1, -1)]
    for device in neighbours:
        pl.semaphore_signal(barrier, inc=1, device_id=device, device_id_type=MESH)

    local_count = [0]
    local_open = []

    def local(src, dst):
        copy = pltpu.make_async_copy(src, dst, s["local_sem"].at[local_count[0]])
        local_count[0] += 1
        copy.start()
        return copy

    small = [
        local(rhs_low, s["rhs_low"]),
        local(inv_ll, s["inv_ll"]),
        local(target, s["target"]),
    ]
    quarter = positions // 4
    lower_in = []
    for d in NEAR_FIRST:
        mine = pl.ds(pl.multiple_of(wrap(y + d) * quarter, quarter), quarter)
        lower_in.append(local(lower.at[:, mine], s["low_in"].at[:, mine]))
    top_in = [
        local(rhs_top.at[pl.ds(pl.multiple_of(c * B, B), B)], s["rhs_top"]),
        local(inv_lt.at[c], s["inv_lt"]),
        local(inv_ut.at[c], s["inv_ut"]),
        local(inv_ul, s["inv_ul"]),
    ]
    upper_in = [
        local(upper.at[:, pl.ds(g * quarter, quarter)], s["up_in"].at[:, pl.ds(g * quarter, quarter)])
        for g in range(4)
    ]

    recv_ids = {}
    sent = [0]
    row_bytes = n * 2

    def recv_sem(key):
        return s["recv_sem"].at[recv_ids.setdefault(key, len(recv_ids))]

    def remote(src, dst, key, device):
        return pltpu.make_async_remote_copy(
            src_ref=src,
            dst_ref=dst,
            send_sem=s["send_sem"].at[len(sent) - 1],
            recv_sem=recv_sem(key),
            device_id=device,
            device_id_type=MESH,
        )

    def send(key, src, dst, device):
        size = math.prod(src.shape) * 2
        if sent[-1] + size > positions * B * row_bytes:
            sent.append(0)
        sent[-1] += size
        remote(src, dst, key, device).start()

    def arrive(key, dst):
        remote(dst, dst, key, partner).wait_recv()

    def wait_sent():
        for i, size in enumerate(sent):
            every = s["fwd"].at[0, pl.ds(0, size // row_bytes)]
            pltpu.make_async_remote_copy(
                src_ref=every,
                dst_ref=every,
                send_sem=s["send_sem"].at[i],
                recv_sem=s["recv_sem"].at[0],
                device_id=partner,
                device_id_type=MESH,
            ).wait_send()

    for copy in small:
        copy.wait()

    targets = s["target"][...]
    order = lax.broadcasted_iota(jnp.int32, targets.shape, 0)
    before, last = jnp.zeros_like(targets), jnp.zeros_like(targets)
    for e in range(slots):
        row = s["target"][e : e + 1, :]
        before = jnp.where((targets == row) & (order > e), e + 1, before)
        last = jnp.where(row == order, e + 1, last)
    s["table"][:slots, :] = before
    s["table"][slots:, :] = last

    def own_rows(row):
        return pl.ds(pl.multiple_of(row * (2 * B), 2 * B), 2 * B)

    def own_half(row, j):
        return pl.ds(pl.multiple_of(row * (2 * B) + j * B, B), B)

    for j in range(2):
        solved = dot(s["inv_ll"][j], s["rhs_low"][pl.ds(j * B, B)]).astype(BF)
        for k in range(GROUPS):
            s["fwd"][k, own_half(r, j)] = solved[:, k * n : (k + 1) * n]

    pl.semaphore_wait(barrier, len(neighbours))

    s["sum_a"][0] = jnp.zeros((B, B), F32)
    s["sum_b"][0] = jnp.zeros((B, B), F32)

    def build(source, arrivals, starts, write):
        def one(acc, m):
            for e in range(slots):
                before = s["tbl"][e, m]
                acc[e + 1] = source[e, m].astype(F32) + acc[before]

        def put(acc, m):
            for q in range(slots):
                last = s["tbl"][slots + q, m]
                write(q, m, acc[last].astype(BF))

        def step(i, carry):
            m0, m1 = i, i + 1
            one(s["sum_a"], m0)
            one(s["sum_b"], m1)
            put(s["sum_a"], m0)
            put(s["sum_b"], m1)
            return carry

        for arrival, start in zip(arrivals, starts):
            arrival.wait()
            if not table_ready:
                table_in.wait()
                table_ready.append(True)
            for half in range(2):
                lax.fori_loop(0, quarter // 4, lambda i, _: step(start + half * 2 + 2 * i, _), 0)
                yield

    def write_low(q, m, value):
        s["low"][q // RING, q % RING, :, pl.ds(pl.multiple_of(m * B, B), B)] = value

    def write_up(q, m, value):
        s["up"][m, :, pl.ds(q * B, B)] = value

    table_in, table_ready = local(s["table"], s["tbl"]), []
    low_build = build(
        s["low_in"], lower_in, [wrap(y + d) * quarter for d in NEAR_FIRST], write_low
    )
    up_build = build(s["up_in"], upper_in, [g * quarter for g in range(4)], write_up)

    built = [0]

    def low_steps():
        for _ in low_build:
            built[0] += 1
            yield

    low_steps = low_steps()

    def ensure(count):
        while built[0] < count:
            next(low_steps)

    def builds():
        yield from low_steps
        yield from up_build

    building = builds()

    def finish(gen):
        for _ in gen:
            pass

    def group(k):
        fwd, solved = s["fwd"].at[k], s["solved"].at[k]
        acc, low_acc = s["acc"].at[k], s["low_acc"].at[k]

        def row_of(d, side):
            return wrap(y + d) * 2 + (core if side == 0 else 1 - core)

        def low_dot(a, d):
            span = pl.ds(pl.multiple_of(wrap(y + d) * (RING * B), RING * B), RING * B)
            rows = s["low"][a, :, :, span].reshape(RING * B, RING * B)
            part = dot(rows, fwd[span]).reshape(RING, B, n)
            acc[a] = part if d == 0 else acc[a] + part

        def low_dots(d):
            ensure(2 * NEAR_FIRST.index(d) + 2)
            arrive((k, "gc", d), fwd.at[own_rows(row_of(d, 1))])

            def step(a, carry):
                low_dot(a, d)
                return carry

            lax.fori_loop(0, RING, step, 0)

        own = fwd.at[own_rows(r)]
        send((k, "gy", 1), own, own, y_at(1))
        send((k, "gy", -1), own, own, y_at(-1))
        send((k, "gc", 0), own, own, partner)
        yield
        before = fwd.at[own_rows(row_of(-1, 0))]
        arrive((k, "gy", 1), before)
        part = fwd.at[own_half(row_of(-1, 0), 0)]
        send((k, "gy2",), part, part, y_at(1))
        send((k, "gc", -1), before, before, partner)
        after = fwd.at[own_rows(row_of(1, 0))]
        arrive((k, "gy", -1), after)
        part = fwd.at[own_half(row_of(1, 0), 1)]
        send((k, "gy2",), part, part, y_at(-1))
        send((k, "gc", 1), after, after, partner)
        yield
        low_dots(0)
        yield
        low_dots(-1)
        beyond = fwd.at[own_rows(row_of(2, 0))]
        arrive((k, "gy2",), beyond)
        send((k, "gc", 2), beyond, beyond, partner)
        yield
        low_dots(1)
        yield
        ensure(2 * RING)
        arrive((k, "gc", 2), fwd.at[own_rows(row_of(2, 1))])

        at_of = ((x_at, z_at), (z_at, x_at))
        cols = (pl.ds(0, w), pl.ds(w, w))

        def place(f, dh, dl):
            if f == 0:
                return wrap(x + dh), wrap(z + dl)
            return wrap(x + dl), wrap(z + dh)

        def mine(f, dh, dl):
            a, b = place(f, dh, dl)
            return acc[a, b, :, cols[f]]

        def far(f, block):
            for i, sides in enumerate(((2, 1), (-1, 0))):
                for t, dl in enumerate(sides):
                    s["far_s"][k, f, i, t] = block(dl).astype(BF)
                d = 1 - 2 * i
                send(
                    (k, "far", f, d), s["far_s"].at[k, f, i], s["far_r"].at[k, f, i], at_of[f][0](d)
                )

        low_dot(wrap(x + 2), 2)
        far(0, lambda dl: mine(0, 2, dl))

        def rest(i, carry):
            low_dot(wrap(x + i - 1), 2)
            return carry

        lax.fori_loop(0, 3, rest, 0)
        far(1, lambda dl: mine(1, 2, dl))
        for f in range(2):
            for i, sides in enumerate(((-1, 0), (2, 1))):
                d = 1 - 2 * i
                for t, dl in enumerate(sides):
                    s["near_s"][k, f, i, t] = mine(f, d, dl).astype(BF)
                send(
                    (k, "ns", f, 1 - i),
                    s["near_s"].at[k, f, i],
                    s["ns_r"].at[k, f, 1 - i, 0],
                    at_of[f][0](d),
                )
        yield
        sides = ((2, 1), (-1, 0))
        for f in range(2):
            for i in range(2):
                d = 1 - 2 * i
                arrive((k, "far", f, d), s["far_r"].at[k, f, i])
                for t, dl in enumerate(sides[i]):
                    total = mine(f, d, dl) + s["far_r"][k, f, i, t].astype(F32)
                    s["sum_s"][k, f, i, t] = total.astype(BF)
                send(
                    (k, "ns", f, i),
                    s["sum_s"].at[k, f, i],
                    s["ns_r"].at[k, f, i, 1],
                    at_of[f][0](d),
                )
        yield
        for f in range(2):
            for i in range(2):
                arrive((k, "ns", f, i), s["ns_r"].at[k, f, i])
                for t, dl in enumerate(sides[i]):
                    total = mine(f, 0, dl) + s["ns_r"][k, f, i, 0, t].astype(F32)
                    total = total + s["ns_r"][k, f, i, 1, t].astype(F32)
                    if dl == 0:
                        s["lsum"][k, f] = total
                        continue
                    u = LIGHT.index(dl)
                    s["light_s"][k, f, u] = total.astype(BF)
                    send(
                        (k, "light", f),
                        s["light_s"].at[k, f, u],
                        s["light_r"].at[k, f, u],
                        at_of[f][1](dl),
                    )
        yield

        if k == 0:
            for copy in top_in:
                copy.wait()

        def block(f, dh, dl):
            a, b = place(f, dh, dl)
            return solved.at[a, b, :, cols[f]]

        passed = {(0, 1), (-1, -1), (1, 1), (2, -1)}

        def spread(f, dl):
            for d in (1, -1):
                key = (k, "pass", f, dl) if (dl, d) in passed else (k, "rest")
                send(key, block(f, 0, dl), block(f, 0, dl), at_of[f][0](d))

        for f in range(2):
            lsum = s["lsum"][k, f]
            arrive((k, "light", f), s["light_r"].at[k, f])
            for u in range(RING - 1):
                lsum = lsum + s["light_r"][k, f, u].astype(F32)
            rhs = s["rhs_top"][:, k * n + f * w : k * n + (f + 1) * w]
            resid_top = (rhs.astype(F32) - lsum).astype(BF)
            fwd_top = dot(s["inv_lt"][...], resid_top).astype(BF)
            solved[x, z, :, cols[f]] = dot(s["inv_ut"][...], fwd_top).astype(BF)
            for d in (2, 1, -1):
                send((k, "sl", f, d), block(f, 0, 0), block(f, 0, 0), at_of[f][1](d))
            spread(f, 0)
        local_open.append(local(solved.at[x, z], out_top.at[:, pl.ds(k * n, n)]))
        yield
        for d in (1, -1, 2):
            for f in range(2):
                arrive((k, "sl", f, d), block(f, 0, -d if d != 2 else 2))
                spread(f, -d if d != 2 else 2)
        yield

        def relay(f, dl, d):
            arrive((k, "pass", f, dl), block(f, -d, dl))
            send((k, "rest"), block(f, -d, dl), block(f, -d, dl), at_of[f][0](d))

        for dl, d in ((0, 1), (-1, -1), (1, 1)):
            for f in range(2):
                relay(f, dl, d)
        yield
        for f in range(2):
            relay(f, 2, -1)
        yield
        finish(building)
        arrive((k, "rest"), solved.at[pl.ds(0, 2)])

        def pair(d):
            i = d % RING
            first = pl.multiple_of(wrap(y + d) * RING, RING)
            rows = s["up"][pl.ds(first, RING)].reshape(RING * B, -1)
            low_acc[i] = dot(rows, solved[...].reshape(-1, n)).reshape(2, 2, B, n)
            s["pair_s"][k, i] = low_acc[i, 1 - core].astype(BF)
            send((k, "pair", d), s["pair_s"].at[k, i], s["pair_r"].at[k, i], partner)

        def paired(d):
            i = d % RING
            arrive((k, "pair", d), s["pair_r"].at[k, i])
            return low_acc[i, core] + s["pair_r"][k, i].astype(F32)

        for d in (2, 1, -1):
            pair(d)
        value = paired(2)
        for j, d in ((0, 1), (1, -1)):
            s["row_far_s"][k, j] = value[j].astype(BF)
            send((k, "yfar", d), s["row_far_s"].at[k, j], s["row_far_r"].at[k, j], y_at(d))
        pair(0)
        for j, d in ((1, 1), (0, -1)):
            low_acc[d % RING, core] = paired(d)
            s["row_near_s"][k, j] = low_acc[d % RING, core, j].astype(BF)
            send((k, "yns", j), s["row_near_s"].at[k, j], s["row_ns_r"].at[k, j, 0], y_at(d))
        yield
        for j, d in ((0, 1), (1, -1)):
            arrive((k, "yfar", d), s["row_far_r"].at[k, j])
            total = low_acc[d % RING, core, j] + s["row_far_r"][k, j].astype(F32)
            s["row_sum_s"][k, j] = total.astype(BF)
            send((k, "yns", j), s["row_sum_s"].at[k, j], s["row_ns_r"].at[k, j, 1], y_at(d))
        low_acc[0, core] = paired(0)
        yield
        for j in range(2):
            arrive((k, "yns", j), s["row_ns_r"].at[k, j])
            usum = low_acc[0, core, j] + s["row_ns_r"][k, j, 0].astype(F32)
            usum = usum + s["row_ns_r"][k, j, 1].astype(F32)
            resid = (fwd[own_half(r, j)].astype(F32) - usum).astype(BF)
            s["out_low"][k, pl.ds(j * B, B)] = dot(s["inv_ul"][j], resid).astype(BF)
        local_open.append(local(s["out_low"].at[k], out_low.at[:, pl.ds(k * n, n)]))

    live = [(k * LAG, group(k)) for k in range(GROUPS)]
    turn = 0
    while live:
        for item in list(live):
            if turn >= item[0] and next(item[1], "done") == "done":
                live.remove(item)
            next(building, None)
        turn += 1
    for copy in local_open:
        copy.wait()
    wait_sent()


def settle(low, top, out_low, out_top, low_buf, top_buf, sem):
    ins = [
        pltpu.make_async_copy(low, low_buf, sem.at[0]),
        pltpu.make_async_copy(top, top_buf, sem.at[1]),
    ]
    outs = [
        pltpu.make_async_copy(low_buf, out_low, sem.at[2]),
        pltpu.make_async_copy(top_buf, out_top, sem.at[3]),
    ]
    for copy in ins:
        copy.start()
    for before, after in zip(ins, outs):
        before.wait()
        after.start()
    for copy in outs:
        copy.wait()


def body(
    rhs_low,
    rhs_top,
    lower_blocks,
    upper_blocks,
    block_target,
    inv_lower_low,
    inv_upper_low,
    inv_lower_top,
    inv_upper_top,
):
    slots, positions, B, _ = lower_blocks.shape
    count = rhs_low.shape[1]
    C, n = GROUPS, rhs_low.shape[1] // GROUPS
    w = n // 2
    VM = pltpu.VMEM

    scratch = {
        "target": VM(block_target.shape, jnp.int32),
        "table": VM((2 * slots, positions), jnp.int32),
        "tbl": pltpu.SMEM((2 * slots, positions), jnp.int32),
        "rhs_low": VM(rhs_low.shape, BF),
        "inv_ll": VM(inv_lower_low.shape, BF),
        "inv_ul": VM(inv_upper_low.shape, BF),
        "rhs_top": VM((B, count), BF),
        "inv_lt": VM((B, B), BF),
        "inv_ut": VM((B, B), BF),
        "low_in": VM(lower_blocks.shape, BF),
        "up_in": VM(upper_blocks.shape, BF),
        "low": VM((RING, RING, B, positions * B), BF),
        "up": VM((positions, B, RING * RING * B), BF),
        "sum_a": VM((slots + 1, B, B), F32),
        "sum_b": VM((slots + 1, B, B), F32),
        "fwd": VM((C, positions * B, n), BF),
        "solved": VM((C, RING, RING, B, n), BF),
        "acc": VM((C, RING, RING, B, n), F32),
        "lsum": VM((C, 2, B, w), F32),
        "low_acc": VM((C, RING, 2, 2, B, n), F32),
        "pair_s": VM((C, RING, 2, B, n), BF),
        "pair_r": VM((C, RING, 2, B, n), BF),
        "out_low": VM((C, 2 * B, n), BF),
        "light_s": VM((C, 2, RING - 1, B, w), BF),
        "light_r": VM((C, 2, RING - 1, B, w), BF),
        **{t: VM((C, 2, 2, 2, B, w), BF) for t in ("far_s", "far_r", "near_s", "sum_s")},
        "ns_r": VM((C, 2, 2, 2, 2, B, w), BF),
        **{t: VM((C, 2, B, n), BF) for t in ("row_far_s", "row_far_r", "row_near_s", "row_sum_s")},
        "row_ns_r": VM((C, 2, 2, B, n), BF),
        "local_sem": pltpu.SemaphoreType.DMA((16 + 2 * C,)),
        "send_sem": pltpu.SemaphoreType.DMA((5 * C,)),
        "recv_sem": pltpu.SemaphoreType.DMA((40 * C,)),
    }
    anywhere = pl.BlockSpec(memory_space=pl.ANY)
    low, top = pl.pallas_call(
        functools.partial(kernel, tuple(scratch)),
        out_shape=(
            jax.ShapeDtypeStruct((2 * B, count), BF),
            jax.ShapeDtypeStruct((B, count), BF),
        ),
        in_specs=[anywhere] * 9,
        out_specs=(anywhere, anywhere),
        scratch_shapes=list(scratch.values()),
        compiler_params=pltpu.CompilerParams(
            collective_id=0, has_side_effects=True, vmem_limit_bytes=66_000_000
        ),
    )(
        block_target,
        rhs_low,
        rhs_top,
        lower_blocks,
        upper_blocks,
        inv_lower_low,
        inv_upper_low,
        inv_lower_top,
        inv_upper_top,
    )
    return pl.pallas_call(
        settle,
        out_shape=(
            jax.ShapeDtypeStruct(low.shape, BF),
            jax.ShapeDtypeStruct(top.shape, BF),
        ),
        in_specs=[anywhere] * 2,
        out_specs=(anywhere, anywhere),
        scratch_shapes=[
            VM(low.shape, BF),
            VM(top.shape, BF),
            pltpu.SemaphoreType.DMA((4,)),
        ],
    )(low, top)


def solution(mesh):
    placed = (
        P(("row", "col"), None),
        P("row", None),
        P("row", "col", None, None),
        P("row", "col", None, None),
        P("row", "col"),
        P(("row", "col"), None, None),
        P(("row", "col"), None, None),
        P("row", None, None),
        P("row", None, None),
    )
    return jax.shard_map(
        body,
        mesh=mesh,
        in_specs=placed,
        out_specs=(P(("row", "col"), None), P(("row", "col"), None)),
        check_vma=False,
    )
```

```python
import functools
import math

import jax
import jax.numpy as jnp
from jax import lax
from jax.experimental import pallas as pl
from jax.experimental.pallas import tpu as pltpu
from jax.sharding import PartitionSpec as P

RING = 4
NEAR_FIRST = (0, -1, 1, 2)
LIGHT = (1, -1, 2)
ORDER = "01" + "b" * 8 + "0011" + "0011" + "01" + "01" + "bbb" + "01" + "bbb" + "01" + "bb" + "01" * 7
GROUPS = 2
BF, F32 = jnp.bfloat16, jnp.float32
MESH = pl.DeviceIdType.MESH


def wrap(i):
    return lax.rem(i + RING, RING)


def dot(a, b):
    return jnp.dot(a, b, preferred_element_type=F32)


def kernel(
    names,
    target,
    rhs_low,
    rhs_top,
    lower,
    upper,
    inv_ll,
    inv_ul,
    inv_lt,
    inv_ut,
    out_low,
    out_top,
    *scratch,
):
    s = dict(zip(names, scratch))
    slots, positions, B, _ = lower.shape
    n = s["fwd"].shape[2]
    w = n // 2
    r, c = lax.axis_index("row"), lax.axis_index("col")
    y, core = lax.div(r, 2), lax.rem(r, 2)
    x, z = lax.div(c, RING), lax.rem(c, RING)
    partner = (y * 2 + 1 - core, c)

    def y_at(d):
        return (wrap(y + d) * 2 + core, c)

    def x_at(d):
        return (r, wrap(x + d) * RING + z)

    def z_at(d):
        return (r, x * RING + wrap(z + d))

    barrier = pltpu.get_barrier_semaphore()
    neighbours = [partner] + [at(d) for at in (y_at, x_at, z_at) for d in (1, -1)]
    for device in neighbours:
        pl.semaphore_signal(barrier, inc=1, device_id=device, device_id_type=MESH)

    local_count = [0]
    local_open = []

    def local(src, dst):
        copy = pltpu.make_async_copy(src, dst, s["local_sem"].at[local_count[0]])
        local_count[0] += 1
        copy.start()
        return copy

    small = [
        local(rhs_low, s["rhs_low"]),
        local(inv_ll, s["inv_ll"]),
        local(target, s["target"]),
    ]
    quarter = positions // 4
    lower_in = []
    for d in NEAR_FIRST:
        mine = pl.ds(pl.multiple_of(wrap(y + d) * quarter, quarter), quarter)
        lower_in.append(local(lower.at[:, mine], s["low_in"].at[:, mine]))
    top_in = [
        local(rhs_top.at[pl.ds(pl.multiple_of(c * B, B), B)], s["rhs_top"]),
        local(inv_lt.at[c], s["inv_lt"]),
        local(inv_ut.at[c], s["inv_ut"]),
        local(inv_ul, s["inv_ul"]),
    ]
    upper_in = [
        local(upper.at[:, pl.ds(g * quarter, quarter)], s["up_in"].at[:, pl.ds(g * quarter, quarter)])
        for g in range(4)
    ]

    recv_ids = {}
    sent = [0]
    row_bytes = n * 2

    def recv_sem(key):
        return s["recv_sem"].at[recv_ids.setdefault(key, len(recv_ids))]

    def remote(src, dst, key, device):
        return pltpu.make_async_remote_copy(
            src_ref=src,
            dst_ref=dst,
            send_sem=s["send_sem"].at[len(sent) - 1],
            recv_sem=recv_sem(key),
            device_id=device,
            device_id_type=MESH,
        )

    def send(key, src, dst, device):
        size = math.prod(src.shape) * 2
        if sent[-1] + size > positions * B * row_bytes:
            sent.append(0)
        sent[-1] += size
        remote(src, dst, key, device).start()

    def arrive(key, dst):
        remote(dst, dst, key, partner).wait_recv()

    def wait_sent():
        for i, size in enumerate(sent):
            every = s["fwd"].at[0, pl.ds(0, size // row_bytes)]
            pltpu.make_async_remote_copy(
                src_ref=every,
                dst_ref=every,
                send_sem=s["send_sem"].at[i],
                recv_sem=s["recv_sem"].at[0],
                device_id=partner,
                device_id_type=MESH,
            ).wait_send()

    for copy in small:
        copy.wait()

    targets = s["target"][...]
    order = lax.broadcasted_iota(jnp.int32, targets.shape, 0)
    before, last = jnp.zeros_like(targets), jnp.zeros_like(targets)
    for e in range(slots):
        row = s["target"][e : e + 1, :]
        before = jnp.where((targets == row) & (order > e), e + 1, before)
        last = jnp.where(row == order, e + 1, last)
    s["table"][:slots, :] = before
    s["table"][slots:, :] = last

    def own_rows(row):
        return pl.ds(pl.multiple_of(row * (2 * B), 2 * B), 2 * B)

    def own_half(row, j):
        return pl.ds(pl.multiple_of(row * (2 * B) + j * B, B), B)

    for j in range(2):
        solved = dot(s["inv_ll"][j], s["rhs_low"][pl.ds(j * B, B)]).astype(BF)
        for k in range(GROUPS):
            s["fwd"][k, own_half(r, j)] = solved[:, k * n : (k + 1) * n]

    pl.semaphore_wait(barrier, len(neighbours))

    s["sum_a"][0] = jnp.zeros((B, B), F32)
    s["sum_b"][0] = jnp.zeros((B, B), F32)

    def build(source, arrivals, starts, write):
        def one(acc, m):
            for e in range(slots):
                before = s["tbl"][e, m]
                acc[e + 1] = source[e, m].astype(F32) + acc[before]

        def put(acc, m):
            for q in range(slots):
                last = s["tbl"][slots + q, m]
                write(q, m, acc[last].astype(BF))

        def step(i, carry):
            m0, m1 = i, i + 1
            one(s["sum_a"], m0)
            one(s["sum_b"], m1)
            put(s["sum_a"], m0)
            put(s["sum_b"], m1)
            return carry

        for arrival, start in zip(arrivals, starts):
            arrival.wait()
            if not table_ready:
                table_in.wait()
                table_ready.append(True)
            for half in range(2):
                lax.fori_loop(0, quarter // 4, lambda i, _: step(start + half * 2 + 2 * i, _), 0)
                yield

    def write_low(q, m, value):
        s["low"][q // RING, q % RING, :, pl.ds(pl.multiple_of(m * B, B), B)] = value

    def write_up(q, m, value):
        s["up"][m, :, pl.ds(q * B, B)] = value

    table_in, table_ready = local(s["table"], s["tbl"]), []
    low_build = build(
        s["low_in"], lower_in, [wrap(y + d) * quarter for d in NEAR_FIRST], write_low
    )
    up_build = build(s["up_in"], upper_in, [g * quarter for g in range(4)], write_up)

    built = [0]

    def low_steps():
        for _ in low_build:
            built[0] += 1
            yield

    low_steps = low_steps()

    def ensure(count):
        while built[0] < count:
            next(low_steps)

    def builds():
        yield from low_steps
        yield from up_build

    building = builds()

    def finish(gen):
        for _ in gen:
            pass

    def group(k):
        fwd, solved = s["fwd"].at[k], s["solved"].at[k]
        acc, low_acc = s["acc"].at[k], s["low_acc"].at[k]

        def row_of(d, side):
            return wrap(y + d) * 2 + (core if side == 0 else 1 - core)

        def low_dot(a, d):
            span = pl.ds(pl.multiple_of(wrap(y + d) * (RING * B), RING * B), RING * B)
            rows = s["low"][a, :, :, span].reshape(RING * B, RING * B)
            part = dot(rows, fwd[span]).reshape(RING, B, n)
            acc[a] = part if d == 0 else acc[a] + part

        def low_dots(d):
            ensure(2 * NEAR_FIRST.index(d) + 2)
            arrive((k, "gc", d), fwd.at[own_rows(row_of(d, 1))])

            def step(a, carry):
                low_dot(a, d)
                return carry

            lax.fori_loop(0, RING, step, 0)

        own = fwd.at[own_rows(r)]
        send((k, "gy", 1), own, own, y_at(1))
        send((k, "gy", -1), own, own, y_at(-1))
        send((k, "gc", 0), own, own, partner)
        yield
        before = fwd.at[own_rows(row_of(-1, 0))]
        arrive((k, "gy", 1), before)
        part = fwd.at[own_half(row_of(-1, 0), 0)]
        send((k, "gy2",), part, part, y_at(1))
        send((k, "gc", -1), before, before, partner)
        after = fwd.at[own_rows(row_of(1, 0))]
        arrive((k, "gy", -1), after)
        part = fwd.at[own_half(row_of(1, 0), 1)]
        send((k, "gy2",), part, part, y_at(-1))
        send((k, "gc", 1), after, after, partner)
        yield
        low_dots(0)
        yield
        low_dots(-1)
        low_dots(1)
        yield
        beyond = fwd.at[own_rows(row_of(2, 0))]
        arrive((k, "gy2",), beyond)
        send((k, "gc", 2), beyond, beyond, partner)
        yield
        ensure(2 * RING)
        arrive((k, "gc", 2), fwd.at[own_rows(row_of(2, 1))])

        at_of = ((x_at, z_at), (z_at, x_at))
        cols = (pl.ds(0, w), pl.ds(w, w))

        def place(f, dh, dl):
            if f == 0:
                return wrap(x + dh), wrap(z + dl)
            return wrap(x + dl), wrap(z + dh)

        def mine(f, dh, dl):
            a, b = place(f, dh, dl)
            return acc[a, b, :, cols[f]]

        def far(f, block):
            for i, sides in enumerate(((2, 1), (-1, 0))):
                for t, dl in enumerate(sides):
                    s["far_s"][k, f, i, t] = block(dl).astype(BF)
                d = 1 - 2 * i
                send(
                    (k, "far", f, d), s["far_s"].at[k, f, i], s["far_r"].at[k, f, i], at_of[f][0](d)
                )

        low_dot(wrap(x + 2), 2)
        far(0, lambda dl: mine(0, 2, dl))

        def rest(i, carry):
            low_dot(wrap(x + i - 1), 2)
            return carry

        lax.fori_loop(0, 3, rest, 0)
        far(1, lambda dl: mine(1, 2, dl))
        for f in range(2):
            for i, sides in enumerate(((-1, 0), (2, 1))):
                d = 1 - 2 * i
                for t, dl in enumerate(sides):
                    s["near_s"][k, f, i, t] = mine(f, d, dl).astype(BF)
                send(
                    (k, "ns", f, 1 - i),
                    s["near_s"].at[k, f, i],
                    s["ns_r"].at[k, f, 1 - i, 0],
                    at_of[f][0](d),
                )
        yield
        sides = ((2, 1), (-1, 0))
        for f in range(2):
            for i in range(2):
                d = 1 - 2 * i
                arrive((k, "far", f, d), s["far_r"].at[k, f, i])
                for t, dl in enumerate(sides[i]):
                    total = mine(f, d, dl) + s["far_r"][k, f, i, t].astype(F32)
                    s["sum_s"][k, f, i, t] = total.astype(BF)
                send(
                    (k, "ns", f, i),
                    s["sum_s"].at[k, f, i],
                    s["ns_r"].at[k, f, i, 1],
                    at_of[f][0](d),
                )
        yield
        for f in range(2):
            for i in range(2):
                arrive((k, "ns", f, i), s["ns_r"].at[k, f, i])
                for t, dl in enumerate(sides[i]):
                    total = mine(f, 0, dl) + s["ns_r"][k, f, i, 0, t].astype(F32)
                    total = total + s["ns_r"][k, f, i, 1, t].astype(F32)
                    if dl == 0:
                        s["lsum"][k, f] = total
                        continue
                    u = LIGHT.index(dl)
                    s["light_s"][k, f, u] = total.astype(BF)
                    send(
                        (k, "light", f),
                        s["light_s"].at[k, f, u],
                        s["light_r"].at[k, f, u],
                        at_of[f][1](dl),
                    )
        yield

        if k == 0:
            for copy in top_in:
                copy.wait()

        def block(f, dh, dl):
            a, b = place(f, dh, dl)
            return solved.at[a, b, :, cols[f]]

        passed = {(0, 1), (-1, -1), (1, 1), (2, -1)}

        def spread(f, dl):
            for d in (1, -1):
                key = (k, "pass", f, dl) if (dl, d) in passed else (k, "keep")
                send(key, block(f, 0, dl), block(f, 0, dl), at_of[f][0](d))

        for f in range(2):
            lsum = s["lsum"][k, f]
            arrive((k, "light", f), s["light_r"].at[k, f])
            for u in range(RING - 1):
                lsum = lsum + s["light_r"][k, f, u].astype(F32)
            rhs = s["rhs_top"][:, k * n + f * w : k * n + (f + 1) * w]
            resid_top = (rhs.astype(F32) - lsum).astype(BF)
            fwd_top = dot(s["inv_lt"][...], resid_top).astype(BF)
            solved[x, z, :, cols[f]] = dot(s["inv_ut"][...], fwd_top).astype(BF)
            for d in (2, 1, -1):
                send((k, "sl", f, d), block(f, 0, 0), block(f, 0, 0), at_of[f][1](d))
            spread(f, 0)
        local_open.append(local(solved.at[x, z], out_top.at[:, pl.ds(k * n, n)]))
        yield
        for d in (1, -1, 2):
            for f in range(2):
                arrive((k, "sl", f, d), block(f, 0, -d if d != 2 else 2))
                spread(f, -d if d != 2 else 2)
        yield

        def relay(f, dl, d):
            arrive((k, "pass", f, dl), block(f, -d, dl))
            send((k, "rest"), block(f, -d, dl), block(f, -d, dl), at_of[f][0](d))

        for dl, d in ((0, 1), (-1, -1), (1, 1)):
            for f in range(2):
                relay(f, dl, d)
        yield
        for f in range(2):
            relay(f, 2, -1)
        yield
        finish(building)

        def low_line(i, blocks, first):
            rows = pl.ds(pl.multiple_of(wrap(y + i) * RING, RING), RING)
            lhs, rhs = [], []
            for dx, dz in blocks:
                a, b = wrap(x + dx), wrap(z + dz)
                span = pl.ds(pl.multiple_of((a * RING + b) * B, B), B)
                lhs.append(s["up"][rows, :, span].reshape(RING * B, B))
                rhs.append(solved[a, b])
            part = dot(jnp.concatenate(lhs, axis=1), jnp.concatenate(rhs, axis=0))
            part = part.reshape(2, 2, B, n)
            low_acc[i] = part if first else low_acc[i] + part

        early = [(dx, dz) for dx in (0, -1, 1) for dz in (0, -1, 1)]
        late = [(dx, dz) for dx in (0, -1, 1, 2) for dz in (0, -1, 1, 2) if 2 in (dx, dz)]
        arrive((k, "keep"), solved.at[0])

        def early_line(i, carry):
            low_line(i, early, True)
            return carry

        lax.fori_loop(0, RING, early_line, 0)
        yield
        arrive((k, "rest"), solved.at[0])

        def pair(d):
            i = d % RING
            low_line(i, late, False)
            s["pair_s"][k, i] = low_acc[i, 1 - core].astype(BF)
            send((k, "pair", d), s["pair_s"].at[k, i], s["pair_r"].at[k, i], partner)

        def paired(d):
            i = d % RING
            arrive((k, "pair", d), s["pair_r"].at[k, i])
            return low_acc[i, core] + s["pair_r"][k, i].astype(F32)

        for d in (2, 1, -1):
            pair(d)
        value = paired(2)
        for j, d in ((0, 1), (1, -1)):
            s["row_far_s"][k, j] = value[j].astype(BF)
            send((k, "yfar", d), s["row_far_s"].at[k, j], s["row_far_r"].at[k, j], y_at(d))
        pair(0)
        for j, d in ((1, 1), (0, -1)):
            low_acc[d % RING, core] = paired(d)
            s["row_near_s"][k, j] = low_acc[d % RING, core, j].astype(BF)
            send((k, "yns", j), s["row_near_s"].at[k, j], s["row_ns_r"].at[k, j, 0], y_at(d))
        yield
        for j, d in ((0, 1), (1, -1)):
            arrive((k, "yfar", d), s["row_far_r"].at[k, j])
            total = low_acc[d % RING, core, j] + s["row_far_r"][k, j].astype(F32)
            s["row_sum_s"][k, j] = total.astype(BF)
            send((k, "yns", j), s["row_sum_s"].at[k, j], s["row_ns_r"].at[k, j, 1], y_at(d))
        low_acc[0, core] = paired(0)
        yield
        for j in range(2):
            arrive((k, "yns", j), s["row_ns_r"].at[k, j])
            usum = low_acc[0, core, j] + s["row_ns_r"][k, j, 0].astype(F32)
            usum = usum + s["row_ns_r"][k, j, 1].astype(F32)
            resid = (fwd[own_half(r, j)].astype(F32) - usum).astype(BF)
            s["out_low"][k, pl.ds(j * B, B)] = dot(s["inv_ul"][j], resid).astype(BF)
        local_open.append(local(s["out_low"].at[k], out_low.at[:, pl.ds(k * n, n)]))

    steps = {"0": group(0), "1": group(1), "b": building}
    for token in ORDER:
        next(steps[token], None)
    for copy in local_open:
        copy.wait()
    wait_sent()


def settle(low, top, out_low, out_top, low_buf, top_buf, sem):
    ins = [
        pltpu.make_async_copy(low, low_buf, sem.at[0]),
        pltpu.make_async_copy(top, top_buf, sem.at[1]),
    ]
    outs = [
        pltpu.make_async_copy(low_buf, out_low, sem.at[2]),
        pltpu.make_async_copy(top_buf, out_top, sem.at[3]),
    ]
    for copy in ins:
        copy.start()
    for before, after in zip(ins, outs):
        before.wait()
        after.start()
    for copy in outs:
        copy.wait()


def body(
    rhs_low,
    rhs_top,
    lower_blocks,
    upper_blocks,
    block_target,
    inv_lower_low,
    inv_upper_low,
    inv_lower_top,
    inv_upper_top,
):
    slots, positions, B, _ = lower_blocks.shape
    count = rhs_low.shape[1]
    C, n = GROUPS, rhs_low.shape[1] // GROUPS
    w = n // 2
    VM = pltpu.VMEM

    scratch = {
        "target": VM(block_target.shape, jnp.int32),
        "table": VM((2 * slots, positions), jnp.int32),
        "tbl": pltpu.SMEM((2 * slots, positions), jnp.int32),
        "rhs_low": VM(rhs_low.shape, BF),
        "inv_ll": VM(inv_lower_low.shape, BF),
        "inv_ul": VM(inv_upper_low.shape, BF),
        "rhs_top": VM((B, count), BF),
        "inv_lt": VM((B, B), BF),
        "inv_ut": VM((B, B), BF),
        "low_in": VM(lower_blocks.shape, BF),
        "up_in": VM(upper_blocks.shape, BF),
        "low": VM((RING, RING, B, positions * B), BF),
        "up": VM((positions, B, RING * RING * B), BF),
        "sum_a": VM((slots + 1, B, B), F32),
        "sum_b": VM((slots + 1, B, B), F32),
        "fwd": VM((C, positions * B, n), BF),
        "solved": VM((C, RING, RING, B, n), BF),
        "acc": VM((C, RING, RING, B, n), F32),
        "lsum": VM((C, 2, B, w), F32),
        "low_acc": VM((C, RING, 2, 2, B, n), F32),
        "pair_s": VM((C, RING, 2, B, n), BF),
        "pair_r": VM((C, RING, 2, B, n), BF),
        "out_low": VM((C, 2 * B, n), BF),
        "light_s": VM((C, 2, RING - 1, B, w), BF),
        "light_r": VM((C, 2, RING - 1, B, w), BF),
        **{t: VM((C, 2, 2, 2, B, w), BF) for t in ("far_s", "far_r", "near_s", "sum_s")},
        "ns_r": VM((C, 2, 2, 2, 2, B, w), BF),
        **{t: VM((C, 2, B, n), BF) for t in ("row_far_s", "row_far_r", "row_near_s", "row_sum_s")},
        "row_ns_r": VM((C, 2, 2, B, n), BF),
        "local_sem": pltpu.SemaphoreType.DMA((16 + 2 * C,)),
        "send_sem": pltpu.SemaphoreType.DMA((5 * C,)),
        "recv_sem": pltpu.SemaphoreType.DMA((42 * C,)),
    }
    anywhere = pl.BlockSpec(memory_space=pl.ANY)
    low, top = pl.pallas_call(
        functools.partial(kernel, tuple(scratch)),
        out_shape=(
            jax.ShapeDtypeStruct((2 * B, count), BF),
            jax.ShapeDtypeStruct((B, count), BF),
        ),
        in_specs=[anywhere] * 9,
        out_specs=(anywhere, anywhere),
        scratch_shapes=list(scratch.values()),
        compiler_params=pltpu.CompilerParams(
            collective_id=0, has_side_effects=True, vmem_limit_bytes=66_000_000
        ),
    )(
        block_target,
        rhs_low,
        rhs_top,
        lower_blocks,
        upper_blocks,
        inv_lower_low,
        inv_upper_low,
        inv_lower_top,
        inv_upper_top,
    )
    return pl.pallas_call(
        settle,
        out_shape=(
            jax.ShapeDtypeStruct(low.shape, BF),
            jax.ShapeDtypeStruct(top.shape, BF),
        ),
        in_specs=[anywhere] * 2,
        out_specs=(anywhere, anywhere),
        scratch_shapes=[
            VM(low.shape, BF),
            VM(top.shape, BF),
            pltpu.SemaphoreType.DMA((4,)),
        ],
    )(low, top)


def solution(mesh):
    placed = (
        P(("row", "col"), None),
        P("row", None),
        P("row", "col", None, None),
        P("row", "col", None, None),
        P("row", "col"),
        P(("row", "col"), None, None),
        P(("row", "col"), None, None),
        P("row", None, None),
        P("row", None, None),
    )
    return jax.shard_map(
        body,
        mesh=mesh,
        in_specs=placed,
        out_specs=(P(("row", "col"), None), P(("row", "col"), None)),
        check_vma=False,
    )
```
